32 devices in a mesh: section: 8 (over z, core), tensor: 4 (over y, x).
Axes of the slice: x: 2, y: 2, z: 4, core: 2. Of those that a mesh axis runs over, the one named last changes fastest.
Arguments:
- fwd_input: float32 [8, 256, 1024], P('section', 'tensor'), may hold values from -6 to 6
- out_grad: float32 [8, 256, 1024], P('section', 'tensor'), may hold values from -6 to 6
- w_inner: float32 [8, 1024, 16384], P('section', None, 'tensor'), may hold values from -0.1875 to 0.1875
- w_outer: float32 [8, 16384, 1024], P('section', 'tensor'), may hold values from -0.046875 to 0.046875
- lent_saved: float32 [8, 256, 16384], P('section', None, 'tensor'), may hold values from -6 to 6
Outputs:
- fwd_output: float32 [8, 256, 1024], P('section', 'tensor')
- in_grad: float32 [8, 256, 1024], P('section', 'tensor')
- lent_new: float32 [8, 256, 16384], P('section', None, 'tensor')
The draws below stay inside these ranges and needn't reach their ends.
All inputs are finite; a program needn't handle non-finite values.
Results may differ from the reference program's by a relative error of at most 0.00007.
Values sent between devices are 32-bit elements; how exact they have to be, the bound alone decides.
A program may use at most 128 MiB of HBM per device.

```python
import jax
import jax.numpy as jnp
from jax import lax

D = 1024
FF = 16384
ROWS = 256
SECTIONS = 8
HALF = 4


def level_of(own_key, dims, shards, smallest, largest):
    def one(position, parts):
        steps = jax.random.uniform(jax.random.fold_in(jax.random.fold_in(own_key, 6), position), (parts,), jnp.float32, smallest / len(shards), largest / len(shards))
        return jnp.repeat(jnp.exp(steps), dims[position] // parts).reshape((-1,) + (1,) * (len(dims) - position - 1))

    gain = one(*shards[0])
    for cut in shards[1:]:
        gain = gain * one(*cut)
    return gain


def bell_draw(own_key, shape, scale, reach, shards=(), kind=jnp.bfloat16):
    loudness = level_of(own_key, shape, shards, -0.22, 0.18) if shards else 1.0
    entries = jax.random.normal(own_key, shape, jnp.float32) * scale * loudness
    return jnp.minimum(jnp.maximum(entries, -reach), reach).astype(kind)


def setup_inputs(seed: int = 0) -> dict:
    streams_of = jax.random.split(jax.random.key(seed), 6)
    return {
        "fwd_input": bell_draw(streams_of[0], (SECTIONS, ROWS, D), 1.0, 6.0, ((0, 8), (1, 4)), jnp.float32),
        "out_grad": bell_draw(streams_of[1], (SECTIONS, ROWS, D), 1.0, 6.0, ((0, 8), (1, 4)), jnp.float32),
        "w_inner": bell_draw(streams_of[2], (SECTIONS, D, FF), D ** -0.5, 0.1875, ((0, 8), (2, 4)), jnp.float32),
        "w_outer": bell_draw(streams_of[3], (SECTIONS, FF, D), FF ** -0.5, 0.046875, ((0, 8), (1, 4)), jnp.float32),
        "lent_saved": bell_draw(streams_of[4], (SECTIONS, ROWS, FF), 1.0, 6.0, ((0, 8), (2, 4)), jnp.float32),
    }


def gelu_exact(value):
    return 0.5 * value * (1.0 + jax.scipy.special.erf(value / jnp.sqrt(2.0).astype(value.dtype)))

def gelu_slope(value):
    cumul = 0.5 * (1.0 + jax.scipy.special.erf(value / jnp.sqrt(2.0).astype(value.dtype)))
    dense = jnp.exp(-0.5 * value * value) / jnp.sqrt(2.0 * jnp.pi).astype(value.dtype)
    return cumul + value * dense

def one_layer(items):
    x_rows, g_rows, w_first, w_second, old_pre = items
    hi = lax.Precision.HIGHEST
    pre = jnp.dot(x_rows, w_first, precision=hi, preferred_element_type=jnp.float32)
    out = x_rows + jnp.dot(gelu_exact(pre), w_second, precision=hi, preferred_element_type=jnp.float32)
    d_act = lax.dot_general(g_rows, w_second, (((1,), (1,)), ((), ())), precision=hi, preferred_element_type=jnp.float32)
    d_pre = d_act * gelu_slope(old_pre)
    grad = g_rows + lax.dot_general(d_pre, w_first, (((1,), (1,)), ((), ())), precision=hi, preferred_element_type=jnp.float32)
    return (out, grad, pre)

def reference(fwd_input, out_grad, w_inner, w_outer, lent_saved):
    old_pre = jnp.roll(lent_saved, -HALF, axis=0)
    outs, grads, pres = lax.map(one_layer, (fwd_input, out_grad, w_inner, w_outer, old_pre))
    fwd_output = jnp.roll(outs, 1, axis=0)
    in_grad = jnp.roll(grads, -1, axis=0)
    lent_new = jnp.roll(pres, -HALF, axis=0)
    return (fwd_output, in_grad, lent_new)
```

```python
import functools

import jax
import jax.numpy as jnp
from jax import lax
from jax.experimental import pallas as pl
from jax.experimental.pallas import tpu as pltpu
from jax.sharding import PartitionSpec as P


OLD_EIGHTHS = (1, 3, 2, 2)
NEW_EIGHTHS = (3, 2, 2, 1)


def across(value, axis, mask):
    pairs = [(source, source ^ mask) for source in range(lax.axis_size(axis))]
    return lax.ppermute(value, axis, pairs)


def from_behind(value, axis, by):
    length = lax.axis_size(axis)
    return lax.ppermute(value, axis, [(i, (i + by) % length) for i in range(length)])


def gelu_exact(value):
    return 0.5 * value * (1.0 + jax.scipy.special.erf(value / jnp.sqrt(2.0).astype(value.dtype)))


def gelu_slope(value):
    cumul = 0.5 * (1.0 + jax.scipy.special.erf(value / jnp.sqrt(2.0).astype(value.dtype)))
    dense = jnp.exp(-0.5 * value * value) / jnp.sqrt(2.0 * jnp.pi).astype(value.dtype)
    return cumul + value * dense


def product(left, right, contract):
    return lax.dot_general(
        left,
        right,
        (contract, ((), ())),
        precision=lax.Precision.HIGHEST,
        preferred_element_type=jnp.float32,
    )


def gather_rows(rows, axis):
    count = lax.axis_size(axis)
    me = lax.axis_index(axis)
    pair, size, width = rows.shape
    whole = jnp.zeros((pair, count * size, width), rows.dtype)
    for d in range(count):
        part = rows if d == 0 else across(rows, axis, d)
        whole = lax.dynamic_update_slice(whole, part, (0, (me ^ d) * size, 0))
    return whole


def scatter_sum(whole, axis):
    count = lax.axis_size(axis)
    me = lax.axis_index(axis)
    size = whole.shape[0] // count
    total = lax.dynamic_slice(whole, (me * size, 0), (size, whole.shape[1]))
    for d in range(1, count):
        part = lax.dynamic_slice(whole, ((me ^ d) * size, 0), (size, whole.shape[1]))
        total = total + across(part, axis, d)
    return total


def moved(value, by):
    half = value.shape[0] // 2
    parts = [from_behind(value[:half], "section", by), from_behind(value[half:], "section", by)]
    return jnp.concatenate(lax.optimization_barrier(parts), axis=0)


def cuts(rows, eighths):
    starts, at = [], 0
    for n in eighths:
        size = rows * n // 8
        starts.append((at, size))
        at += size
    return starts


def put_kernel(at, *refs):
    part, out, sem = refs[-3:]
    copy = pltpu.make_async_copy(part, out.at[0, pl.ds(at, part.shape[0])], sem)
    copy.start()
    copy.wait()


def put(whole, part, at, shape):
    anywhere = pl.BlockSpec(memory_space=pl.ANY)
    held = () if whole is None else (whole,)
    return pl.pallas_call(
        functools.partial(put_kernel, at),
        out_shape=jax.ShapeDtypeStruct(shape, part.dtype),
        in_specs=[anywhere] * len(held) + [pl.BlockSpec(memory_space=pltpu.VMEM)],
        out_specs=anywhere,
        scratch_shapes=[pltpu.SemaphoreType.DMA],
        input_output_aliases={0: 0} if held else {},
        cost_estimate=pl.CostEstimate(flops=0, bytes_accessed=2 * part.size * 4, transcendentals=0),
    )(*held, part)


def shards(fwd_input, out_grad, w_inner, w_outer, lent_saved):
    x_rows = fwd_input[0]
    g_rows = out_grad[0]
    w_first = w_inner[0]
    w_second = w_outer[0]
    held = lent_saved[0]
    mask = lax.axis_size("section") // 2
    rows, width = held.shape
    barrier = lax.optimization_barrier

    old = []
    for i, (at, size) in enumerate(cuts(rows, OLD_EIGHTHS)):
        piece = held[at : at + size]
        if i == 0:
            piece, held = barrier((piece, held))
        old.append(across(piece, "section", mask))

    both = gather_rows(jnp.stack([x_rows, g_rows]), "tensor")

    pre = product(both[0], w_first, ((1,), (0,)))
    summed = scatter_sum(product(gelu_exact(pre), w_second, ((1,), (0,))), "tensor")
    moved_out = moved(x_rows + summed, 1)

    d_act = product(both[1], w_second, ((1,), (1,)))
    d_pre = d_act * gelu_slope(jnp.concatenate(old, axis=0))
    summed = scatter_sum(product(d_pre, w_first, ((1,), (1,))), "tensor")
    moved_grad = moved(g_rows + summed, -1)

    given = None
    shape = (1, rows, width)
    spans = cuts(rows, NEW_EIGHTHS)
    last = len(spans) - 1
    flying = []
    for i, (at, size) in enumerate(spans):
        piece = pre[at : at + size]
        if i == 1:
            piece, _ = barrier((piece, old))
        elif i >= 2:
            place, part = flying[i - 2]
            given = put(given, part, place, shape)
            if i == last:
                piece, given, moved_out, moved_grad = barrier((piece, given, moved_out, moved_grad))
            else:
                piece, given = barrier((piece, given))
        flying.append((at, across(piece, "section", mask)))
    for place, part in flying[-2:]:
        given = put(given, part, place, shape)
    return (moved_out[None], moved_grad[None], given)


def solution(mesh):
    return jax.shard_map(
        shards,
        mesh=mesh,
        in_specs=(
            P("section", "tensor", None),
            P("section", "tensor", None),
            P("section", None, "tensor"),
            P("section", "tensor", None),
            P("section", None, "tensor"),
        ),
        out_specs=(
            P("section", "tensor", None),
            P("section", "tensor", None),
            P("section", None, "tensor"),
        ),
        check_vma=False,
    )
```

```python
import functools

import jax
import jax.numpy as jnp
from jax import lax
from jax.experimental import pallas as pl
from jax.experimental.pallas import tpu as pltpu
from jax.sharding import PartitionSpec as P


NEW_EIGHTHS = (4, 3, 1)


def across(value, axis, mask):
    pairs = [(source, source ^ mask) for source in range(lax.axis_size(axis))]
    return lax.ppermute(value, axis, pairs)


def from_behind(value, axis, by):
    length = lax.axis_size(axis)
    return lax.ppermute(value, axis, [(i, (i + by) % length) for i in range(length)])


def gelu_exact(value):
    return 0.5 * value * (1.0 + jax.scipy.special.erf(value / jnp.sqrt(2.0).astype(value.dtype)))


def gelu_slope(value):
    cumul = 0.5 * (1.0 + jax.scipy.special.erf(value / jnp.sqrt(2.0).astype(value.dtype)))
    dense = jnp.exp(-0.5 * value * value) / jnp.sqrt(2.0 * jnp.pi).astype(value.dtype)
    return cumul + value * dense


def product(left, right, contract):
    return lax.dot_general(
        left,
        right,
        (contract, ((), ())),
        precision=lax.Precision.HIGHEST,
        preferred_element_type=jnp.float32,
    )


def gather_rows(rows, axis):
    count = lax.axis_size(axis)
    me = lax.axis_index(axis)
    pair, size, width = rows.shape
    whole = jnp.zeros((pair, count * size, width), rows.dtype)
    for d in range(count):
        part = rows if d == 0 else across(rows, axis, d)
        whole = lax.dynamic_update_slice(whole, part, (0, (me ^ d) * size, 0))
    return whole


def scatter_sum(whole, axis):
    count = lax.axis_size(axis)
    me = lax.axis_index(axis)
    size = whole.shape[0] // count
    total = lax.dynamic_slice(whole, (me * size, 0), (size, whole.shape[1]))
    for d in range(1, count):
        part = lax.dynamic_slice(whole, ((me ^ d) * size, 0), (size, whole.shape[1]))
        total = total + across(part, axis, d)
    return total


def moved(value, by):
    half = value.shape[0] // 2
    parts = [from_behind(value[:half], "section", by), from_behind(value[half:], "section", by)]
    return jnp.concatenate(lax.optimization_barrier(parts), axis=0)


def cuts(rows, eighths):
    starts, at = [], 0
    for n in eighths:
        size = rows * n // 8
        starts.append((at, size))
        at += size
    return starts


def put_kernel(at, *refs):
    part, out, sem = refs[-3:]
    copy = pltpu.make_async_copy(part, out.at[0, pl.ds(at, part.shape[0])], sem)
    copy.start()
    copy.wait()


def put(whole, part, at, shape):
    anywhere = pl.BlockSpec(memory_space=pl.ANY)
    held = () if whole is None else (whole,)
    return pl.pallas_call(
        functools.partial(put_kernel, at),
        out_shape=jax.ShapeDtypeStruct(shape, part.dtype),
        in_specs=[anywhere] * len(held) + [pl.BlockSpec(memory_space=pltpu.VMEM)],
        out_specs=anywhere,
        scratch_shapes=[pltpu.SemaphoreType.DMA],
        input_output_aliases={0: 0} if held else {},
        cost_estimate=pl.CostEstimate(flops=0, bytes_accessed=2 * part.size * 4, transcendentals=0),
    )(*held, part)


def shards(fwd_input, out_grad, w_inner, w_outer, lent_saved):
    x_rows = fwd_input[0]
    g_rows = out_grad[0]
    w_first = w_inner[0]
    w_second = w_outer[0]
    held = lent_saved[0]
    mask = lax.axis_size("section") // 2
    rows, width = held.shape
    barrier = lax.optimization_barrier

    old_pre = across(held, "section", mask)

    both = gather_rows(jnp.stack([x_rows, g_rows]), "tensor")
    x_all, g_all = both[0], both[1]

    d_act = product(g_all, w_second, ((1,), (1,)))
    x_all, d_act = barrier((x_all, d_act))

    pre = product(x_all, w_first, ((1,), (0,)))
    summed = product(gelu_exact(pre), w_second, ((1,), (0,)))
    moved_out = moved(x_rows + scatter_sum(summed, "tensor"), 1)

    spans = cuts(rows, NEW_EIGHTHS)
    flying = []
    for i, (at, size) in enumerate(spans):
        piece = pre[at : at + size]
        if i >= 1:
            piece, old_pre = barrier((piece, old_pre))
        flying.append((at, across(piece, "section", mask)))

    d_pre = d_act * gelu_slope(old_pre)
    summed = product(d_pre, w_first, ((1,), (1,)))
    moved_grad = moved(g_rows + scatter_sum(summed, "tensor"), -1)

    given = None
    for place, part in flying[:-1]:
        given = put(given, part, place, (1, rows, width))
    given, moved_out, moved_grad = barrier((given, moved_out, moved_grad))
    place, part = flying[-1]
    given = lax.dynamic_update_slice(given, part[None], (0, place, 0))
    return (moved_out[None], moved_grad[None], given)


def solution(mesh):
    return jax.shard_map(
        shards,
        mesh=mesh,
        in_specs=(
            P("section", "tensor", None),
            P("section", "tensor", None),
            P("section", None, "tensor"),
            P("section", "tensor", None),
            P("section", None, "tensor"),
        ),
        out_specs=(
            P("section", "tensor", None),
            P("section", "tensor", None),
            P("section", None, "tensor"),
        ),
        check_vma=False,
    )
```
